32 devices in a mesh: row: 4 (over z), col: 2 (over y), ex: 4 (over x, core).
Axes of the slice: x: 2, y: 2, z: 4, core: 2. Of those that a mesh axis runs over, the one named last changes fastest.
Arguments:
- train_in: bfloat16 [2048, 8192], P('ex', 'row'), may hold values from -6 to 6
- train_out: bfloat16 [2048, 8192], P('ex', 'col'), may hold values from -0.0047912598 to 0.0047912598
- query_in: bfloat16 [128, 8192], P('ex', 'row'), may hold values from -6 to 6
- query_out: bfloat16 [128, 8192], P('ex', 'col'), may hold values from -0.023925781 to 0.023925781
- query_ids: int32 [128], P('ex'), may hold values from 0 to 1
- in_basis: bfloat16 [8, 1024, 1024], P('row'), may hold values from -1 to 1, as said below
- out_basis: bfloat16 [8, 1024, 1024], P('col'), may hold values from -1 to 1, as said below
- level_table: float32 [64, 64], replicated, may hold values from 0.5 to 8
- in_level: int32 [8192], P('row'), may hold values from 0 to 63
- out_level: int32 [8192], P('col'), may hold values from 0 to 63
- lengths: int32 [4], replicated, may hold values from 1 to 1024, 2048 in all
Outputs:
- token_scores: float32 [2, 2048], P(None, 'ex')
- example_scores: float32 [2, 4], replicated
The draws below stay inside these ranges and needn't reach their ends.
Inputs may be any that keep to these rules, and one draw needn't show every extreme that they name: `in_basis`: each block is an orthogonal matrix rounded to bfloat16. `out_basis`: each block is an orthogonal matrix rounded to bfloat16. `lengths`: the counts sum to 2048.
All inputs are finite; a program needn't handle non-finite values.
Results may differ from the reference program's by a relative error of at most 0.018.
Values may be sent and summed in bfloat16 or wider, within the bound.
A program may use at most 192 MiB of HBM per device.

```python
import math
import jax
import jax.numpy as jnp
import numpy as np
from jax import lax

D_IN = 8192
D_OUT = 8192
BLOCK = 1024
QUERIES = 2
LEVELS = 64
EXAMPLES = 4
TOKENS = 2048
QTOKENS = 128
MOSTLEN = 1024
IN_BLOCKS = 8
OUT_BLOCKS = 8


def orthogonal_blocks(key, count):
    normal = jax.random.normal(key, (count, BLOCK, BLOCK), jnp.float32)
    factor, upper = jnp.linalg.qr(normal)
    return factor


def draw_in_basis(key, part):
    return orthogonal_blocks(jax.random.fold_in(key, 11), IN_BLOCKS).astype(jnp.bfloat16)


def draw_out_basis(key, part):
    return orthogonal_blocks(jax.random.fold_in(key, 23), OUT_BLOCKS).astype(jnp.bfloat16)


def place_ends(result, own_key, smallest, high):
    dims = result.shape
    index_at = [jax.random.randint(jax.random.fold_in(own_key, axis), (), 0, dims[axis]) for axis in range(len(dims))]
    result = result.at[tuple(index_at)].set(smallest)
    longest = dims.index(max(dims))
    index_at[longest] = (index_at[longest] + 1) % dims[longest]
    return result.at[tuple(index_at)].set(high)


def levels(rng, shape, cuts, least, top_value):
    factor_of = 1.0
    for axis_at, parts in cuts:
        heights = jax.random.uniform(jax.random.fold_in(jax.random.fold_in(rng, 6), axis_at), (parts,), jnp.float32, least / len(cuts), top_value / len(cuts))
        factor_of = factor_of * jnp.repeat(jnp.exp(heights), shape[axis_at] // parts).reshape((-1,) + (1,) * (len(shape) - 1 - axis_at))
    return factor_of


def split_up(amount, total, bound, lean):
    weights = [(1 << 20) // math.isqrt(standing ** lean) + 1 for standing in range(2, amount + 1)]
    surplus, given = total - bound - (amount - 1), [1] * (amount - 1)
    while surplus > 0:
        movable = [i for i in range(amount - 1) if given[i] < bound]
        whole, remaining = sum([weights[i] for i in movable]), surplus
        for i in movable:
            extra = min(bound - given[i], max(1, remaining * weights[i] // whole), surplus)
            given[i] = given[i] + extra
            surplus = surplus - extra
    return np.array([bound] + given)


def uneven(own_key, number_of, total, bound, slope):
    if number_of == 2:
        one = jax.random.randint(own_key, (), max(1, total - bound), min(bound, total - 1) + 1)
        return jnp.stack([one, total - one])
    tallies = jnp.asarray(split_up(number_of, total, bound, slope), jnp.int32)
    pairs = (number_of - 1) // 2
    source_of, sink = tallies[1:1 + 2 * pairs:2], tallies[2:2 + 2 * pairs:2]
    room = jnp.minimum(source_of - 1, bound - sink)
    shifted = jax.random.randint(jax.random.fold_in(own_key, 1), (pairs,), 0, 1 << 20) % (room + 1)
    tallies = tallies.at[1:1 + 2 * pairs:2].set(source_of - shifted).at[2:2 + 2 * pairs:2].set(sink + shifted)
    return tallies[jax.random.permutation(jax.random.fold_in(own_key, 2), number_of)]


def gaussian(own_key, dims, spread, limit, pieces=(), kind=jnp.bfloat16):
    values = jax.random.normal(own_key, dims, jnp.float32) * spread
    if len(pieces) > 0:
        values = levels(own_key, dims, pieces, -0.22, 0.18) * values
    return jnp.clip(values, min=-limit, max=limit).astype(kind)


def setup_inputs(seed: int = 0) -> dict:
    splits = jax.random.split(jax.random.key(seed), 12)
    return {
        "train_in": gaussian(splits[0], (TOKENS, D_IN), 1.0, 6.0, ((0, 4), (1, 4))),
        "train_out": gaussian(splits[1], (TOKENS, D_OUT), 0.0008, 0.0047912598, ((0, 4), (1, 2))),
        "query_in": gaussian(splits[2], (QTOKENS, D_IN), 1.0, 6.0, ((0, 4), (1, 4))),
        "query_out": gaussian(splits[3], (QTOKENS, D_OUT), 0.004, 0.023925781, ((0, 4), (1, 2))),
        "query_ids": place_ends(jax.random.randint(splits[4], (QTOKENS,), 0, QUERIES), jax.random.fold_in(splits[4], 1), 0, QUERIES - 1).astype(jnp.int32),
        "in_basis": draw_in_basis(jax.random.fold_in(splits[11], 71), 0),
        "out_basis": draw_out_basis(jax.random.fold_in(splits[11], 71), 0),
        "level_table": jnp.clip(jnp.exp(jax.random.uniform(splits[7], (LEVELS, LEVELS), jnp.float32, math.log(0.5), math.log(8.0))), 0.5, 8.0),
        "in_level": place_ends(jax.random.randint(splits[8], (D_IN,), 0, LEVELS), jax.random.fold_in(splits[8], 1), 0, LEVELS - 1).astype(jnp.int32),
        "out_level": place_ends(jax.random.randint(splits[9], (D_OUT,), 0, LEVELS), jax.random.fold_in(splits[9], 1), 0, LEVELS - 1).astype(jnp.int32),
        "lengths": uneven(splits[10], EXAMPLES, TOKENS, MOSTLEN, 2).astype(jnp.int32),
    }


DAMPING = 0.1

def rounded(value):
    return lax.optimization_barrier(value.astype(jnp.bfloat16)).astype(jnp.float32)

def reference(train_in, train_out, query_in, query_out, query_ids, in_basis, out_basis, level_table, in_level, out_level, lengths):
    highest = lax.Precision.HIGHEST
    q_in = query_in.astype(jnp.float32)
    q_out = query_out.astype(jnp.float32)
    basis_out = out_basis.astype(jnp.float32)
    basis_in = in_basis.astype(jnp.float32)
    eigen = level_table[out_level[:, None], in_level[None, :]].reshape(OUT_BLOCKS, BLOCK, IN_BLOCKS, BLOCK)
    acts = train_in.astype(jnp.float32)
    grads = train_out.astype(jnp.float32)

    def per_query(query):
        weights = (query_ids == query).astype(jnp.float32)
        grad = jnp.dot((q_out * weights[:, None]).T, q_in, precision=highest)
        grad = rounded(grad).reshape(OUT_BLOCKS, BLOCK, IN_BLOCKS, BLOCK)
        half = rounded(jnp.einsum('iab,iajc->ibjc', basis_out, grad, precision=highest))
        rotated = jnp.einsum('ibjc,jcd->ibjd', half, basis_in, precision=highest)
        damped = rounded(rotated / (eigen + DAMPING))
        back = rounded(jnp.einsum('ibjd,jcd->ibjc', damped, basis_in, precision=highest))
        precond = rounded(jnp.einsum('iab,ibjc->iajc', basis_out, back, precision=highest))
        precond = precond.reshape(D_OUT, D_IN)
        image = jnp.dot(acts, precond.T, precision=highest)
        return jnp.sum(image * grads, axis=1)
    token_scores = lax.map(per_query, jnp.arange(QUERIES, dtype=jnp.int32))
    ends = jnp.cumsum(lengths).astype(jnp.int32)
    starts = (ends - lengths).astype(jnp.int32)
    positions = jnp.arange(TOKENS, dtype=jnp.int32)
    member = ((positions[None, :] >= starts[:, None]) & (positions[None, :] < ends[:, None])).astype(jnp.float32)
    example_scores = jnp.dot(token_scores, member.T, precision=highest)
    return (token_scores, example_scores)
```

```python
import functools

import jax
import jax.numpy as jnp
from jax import lax
from jax.experimental import pallas as pl
from jax.experimental.pallas import tpu as pltpu
from jax.sharding import PartitionSpec as P

QUERIES = 2
DAMPING = 0.1
MESH = pl.DeviceIdType.MESH
F32 = jnp.float32
BF16 = jnp.bfloat16


def dot(a, b):
    return jnp.dot(a, b, preferred_element_type=F32)


def kernel(
    sizes,
    train_in,
    train_out,
    query_in,
    query_out,
    ids,
    in_basis,
    out_basis,
    table_ref,
    in_level,
    out_level,
    lengths,
    token_out,
    example_out,
    acts,
    grads,
    basis_in,
    basis_out,
    q_in,
    q_out,
    q_ids,
    hot_t,
    inverse,
    left,
    right,
    damp0,
    damp1,
    acc0,
    acc1,
    lanes,
    parts,
    sums,
    load_sem,
    q_load_sem,
    q_send_sem,
    q_fwd_sem,
    q_recv_sem,
    part_send,
    part_recv,
    sum_send,
    sum_recv,
):
    rows, cols, exs, tile = sizes
    row, col, ex = lax.axis_index("row"), lax.axis_index("col"), lax.axis_index("ex")
    in_sub, width, _ = in_basis.shape
    out_sub = out_basis.shape[0]
    tokens = train_in.shape[0]
    held = query_in.shape[0]
    group = rows * cols
    place = row * cols + col
    chips = exs // 2
    sibling = ex + 1 - 2 * lax.rem(ex, 2)

    def ex_peer(k):
        return lax.rem(ex + k, exs)

    def group_peer(k):
        other = lax.rem(place + k, group)
        return {"row": other // cols, "col": lax.rem(other, cols)}

    def slot(ref, e):
        return ref.at[pl.ds(pl.multiple_of(e * held, held), held), :]

    own = [
        pltpu.make_async_copy(src, slot(ref, ex), q_load_sem.at[n])
        for n, (src, ref) in enumerate(((ids, q_ids), (query_in, q_in), (query_out, q_out)))
    ]
    for copy in own:
        copy.start()
    in_loads, out_loads = [], []
    for j in range(in_sub):
        in_loads.append(
            (
                pltpu.make_async_copy(
                    train_in.at[:, pl.ds(j * width, width)], acts.at[j], load_sem.at[0, 0, j]
                ),
                pltpu.make_async_copy(in_basis.at[j], basis_in.at[j], load_sem.at[0, 1, j]),
            )
        )
    for i in range(out_sub):
        out_loads.append(
            (
                pltpu.make_async_copy(
                    train_out.at[:, pl.ds(i * width, width)], grads.at[i], load_sem.at[1, 0, i]
                ),
                pltpu.make_async_copy(out_basis.at[i], basis_out.at[i], load_sem.at[1, 1, i]),
            )
        )
    for pair in in_loads + out_loads:
        for copy in pair:
            copy.start()

    barrier = pltpu.get_barrier_semaphore()
    for k in range(1, exs):
        pl.semaphore_signal(barrier, inc=1, device_id={"ex": ex_peer(k)}, device_id_type=MESH)
    for k in range(1, group):
        pl.semaphore_signal(barrier, inc=1, device_id=group_peer(k), device_id_type=MESH)
    pl.semaphore_wait(barrier, exs - 1 + group - 1)

    gathered = (q_ids, q_in, q_out)

    def move(n, e, to, send):
        return pltpu.make_async_remote_copy(
            src_ref=slot(gathered[n], e),
            dst_ref=slot(gathered[n], e),
            send_sem=send,
            recv_sem=q_recv_sem.at[n, e],
            device_id={"ex": to},
            device_id_type=MESH,
        )

    firsts = []
    for n in range(3):
        own[n].wait()
        for k in range(1, chips):
            firsts.append(move(n, ex, ex_peer(2 * k), q_send_sem.at[n, k]))
        firsts.append(move(n, ex, sibling, q_send_sem.at[n, 0]))
    for copy in firsts:
        copy.start()

    for j in range(in_sub):
        for copy in in_loads[j]:
            copy.wait()
        acts[j] = dot(acts[j], basis_in[j]).astype(BF16)
    for i in range(out_sub):
        for copy in out_loads[i]:
            copy.wait()
        grads[i] = dot(grads[i], basis_out[i]).astype(BF16)

    forwards = []
    for n in range(3):
        for k in range(1, chips):
            source = lax.rem(ex + exs - 2 * k, exs)
            move(n, source, sibling, q_fwd_sem.at[n, k]).wait_recv()
            forwards.append(move(n, source, sibling, q_fwd_sem.at[n, k]))
            forwards[-1].start()

    table = 1.0 / (table_ref[...] + DAMPING)
    levels = table.shape[0]
    high = table.astype(BF16)
    low = (table - high.astype(F32)).astype(BF16)
    split = jnp.concatenate([high.astype(F32), low.astype(F32)], axis=0).astype(BF16)
    n_in, n_out = in_sub * width, out_sub * width
    in_hot = (
        lax.broadcasted_iota(jnp.int32, (levels, n_in), 0) == in_level[...]
    ).astype(F32).astype(BF16)
    spread = dot(split, in_hot).astype(BF16)
    for i in range(out_sub):
        out_hot = (
            lax.rem(lax.broadcasted_iota(jnp.int32, (2 * levels, width), 0), levels)
            == out_level[:, pl.ds(i * width, width)]
        ).astype(F32)
        hot_t[pl.ds(i * width, width), :] = out_hot.T.astype(BF16)
    step = width // 4

    def expand(k, carry):
        at = pl.ds(pl.multiple_of(k * step, step), step)
        inverse[at, :] = dot(hot_t[at, :], spread).astype(BF16)
        return carry

    lax.fori_loop(0, n_out // step, expand, 0)

    for n in range(3):
        move(n, sibling, sibling, q_send_sem.at[n, 0]).wait_recv()
        for k in range(1, chips):
            source = lax.rem(sibling + exs - 2 * k, exs)
            move(n, source, sibling, q_send_sem.at[n, 0]).wait_recv()
    for copy in firsts + forwards:
        copy.wait_send()

    count = exs * held
    who = q_ids[:, 0:1]
    for j in range(in_sub):
        turned = dot(q_in[:, pl.ds(j * width, width)], basis_in[j])
        for q in range(QUERIES):
            right[q, :, pl.ds(j * width, width)] = jnp.where(who == q, turned, 0.0).astype(BF16)
    for i in range(out_sub):
        turned = dot(q_out[:, pl.ds(i * width, width)], basis_out[i])
        left[pl.ds(i * width, width), :] = turned.T.astype(BF16)

    damps, accs = (damp0, damp1), (acc0, acc1)
    lanes[...] = jnp.zeros_like(lanes)
    tiles = n_in // tile
    per = width // tile

    def build(q, n):
        c, i = n // out_sub, lax.rem(n, out_sub)
        at_c = pl.ds(pl.multiple_of(c * tile, tile), tile)
        at_r = pl.ds(pl.multiple_of(i * width, width), width)
        rotated = dot(left[at_r, :], right[q, :, at_c])
        damps[q][...] = (rotated * inverse[at_r, at_c].astype(F32)).astype(BF16)

    def outer(c, carry):
        for q in range(QUERIES):
            accs[q][...] = jnp.zeros_like(accs[q])

        def inner(i, carry):
            n = c * out_sub + i
            build(1, n)
            accs[0][...] += dot(grads[i], damp0[...])
            build(0, jnp.minimum(n + 1, tiles * out_sub - 1))
            accs[1][...] += dot(grads[i], damp1[...])
            return carry

        lax.fori_loop(0, out_sub, inner, 0)
        x = acts[c // per, :, pl.ds(pl.multiple_of(lax.rem(c, per) * tile, tile), tile)].astype(F32)
        for q in range(QUERIES):
            product = accs[q][...] * x
            total = product[:, 0:128]
            for g in range(1, tile // 128):
                total = total + product[:, g * 128 : (g + 1) * 128]
            lanes[q] += total
        return carry

    build(0, 0)
    lax.fori_loop(0, tiles, outer, 0)

    mine = jnp.concatenate(
        [jnp.sum(lanes[q].T, axis=0, keepdims=True) for q in range(QUERIES)], axis=0
    )
    parts[place] = mine
    sends = []
    for k in range(1, group):
        sends.append(
            pltpu.make_async_remote_copy(
                src_ref=parts.at[place],
                dst_ref=parts.at[place],
                send_sem=part_send.at[k],
                recv_sem=part_recv.at[place],
                device_id=group_peer(k),
                device_id_type=MESH,
            )
        )
        sends[-1].start()
    for k in range(1, group):
        source = lax.rem(place + k, group)
        pltpu.make_async_remote_copy(
            src_ref=parts.at[source],
            dst_ref=parts.at[source],
            send_sem=part_send.at[k],
            recv_sem=part_recv.at[source],
            device_id=group_peer(k),
            device_id_type=MESH,
        ).wait_recv()
    for copy in sends:
        copy.wait_send()
    scores = jnp.sum(parts[...], axis=0)
    token_out[...] = scores

    position = ex * tokens + lax.broadcasted_iota(jnp.int32, (QUERIES, tokens), 1)
    lane = lax.broadcasted_iota(jnp.int32, (QUERIES, 128), 1)
    found = jnp.zeros((QUERIES, 128), F32)
    start = jnp.int32(0)
    for e in range(lengths.shape[0]):
        end = start + lengths[e]
        inside = (position >= start) & (position < end)
        value = jnp.sum(jnp.where(inside, scores, 0.0), axis=1, keepdims=True)
        found = jnp.where(lane == e, value, found)
        start = end
    sums[ex] = found
    sends = []
    for k in range(1, exs):
        sends.append(
            pltpu.make_async_remote_copy(
                src_ref=sums.at[ex],
                dst_ref=sums.at[ex],
                send_sem=sum_send.at[k],
                recv_sem=sum_recv.at[ex],
                device_id={"ex": ex_peer(k)},
                device_id_type=MESH,
            )
        )
        sends[-1].start()
    for k in range(1, exs):
        source = ex_peer(k)
        pltpu.make_async_remote_copy(
            src_ref=sums.at[source],
            dst_ref=sums.at[source],
            send_sem=sum_send.at[k],
            recv_sem=sum_recv.at[source],
            device_id={"ex": source},
            device_id_type=MESH,
        ).wait_recv()
    for copy in sends:
        copy.wait_send()
    example_out[...] = jnp.sum(sums[...], axis=0)[:, 0 : lengths.shape[0]]


def solution(mesh):
    rows, cols, exs = mesh.shape["row"], mesh.shape["col"], mesh.shape["ex"]

    def body(
        train_in,
        train_out,
        query_in,
        query_out,
        query_ids,
        in_basis,
        out_basis,
        level_table,
        in_level,
        out_level,
        lengths,
    ):
        in_sub, width, _ = in_basis.shape
        out_sub = out_basis.shape[0]
        tokens, held = train_in.shape[0], query_in.shape[0]
        count = exs * held
        n_in, n_out = in_sub * width, out_sub * width
        levels = level_table.shape[0]
        tile = width // 2
        group = rows * cols
        ids = jnp.broadcast_to(query_ids[:, None], (held, 128))
        hbm = pl.BlockSpec(memory_space=pl.ANY)
        vmem = pl.BlockSpec(memory_space=pltpu.VMEM)
        smem = pl.BlockSpec(memory_space=pltpu.SMEM)
        most = max(in_sub, out_sub)
        dma = pltpu.SemaphoreType.DMA
        return pl.pallas_call(
            functools.partial(kernel, (rows, cols, exs, tile)),
            out_shape=(
                jax.ShapeDtypeStruct((QUERIES, tokens), F32),
                jax.ShapeDtypeStruct((QUERIES, lengths.shape[0]), F32),
            ),
            in_specs=[hbm] * 7 + [vmem] * 3 + [smem],
            out_specs=(vmem, vmem),
            scratch_shapes=[
                pltpu.VMEM((in_sub, tokens, width), BF16),
                pltpu.VMEM((out_sub, tokens, width), BF16),
                pltpu.VMEM((in_sub, width, width), BF16),
                pltpu.VMEM((out_sub, width, width), BF16),
                pltpu.VMEM((count, n_in), BF16),
                pltpu.VMEM((count, n_out), BF16),
                pltpu.VMEM((count, 128), jnp.int32),
                pltpu.VMEM((n_out, 2 * levels), BF16),
                pltpu.VMEM((n_out, n_in), BF16),
                pltpu.VMEM((n_out, count), BF16),
                pltpu.VMEM((QUERIES, count, n_in), BF16),
                pltpu.VMEM((width, tile), BF16),
                pltpu.VMEM((width, tile), BF16),
                pltpu.VMEM((tokens, tile), F32),
                pltpu.VMEM((tokens, tile), F32),
                pltpu.VMEM((QUERIES, tokens, 128), F32),
                pltpu.VMEM((group, QUERIES, tokens), F32),
                pltpu.VMEM((exs, QUERIES, 128), F32),
                dma((2, 2, most)),
                dma((3,)),
                dma((3, exs // 2)),
                dma((3, exs // 2)),
                dma((3, exs)),
                dma((group,)),
                dma((group,)),
                dma((exs,)),
                dma((exs,)),
            ],
            compiler_params=pltpu.CompilerParams(
                collective_id=0, has_side_effects=True, vmem_limit_bytes=66 * 1000 * 1000
            ),
        )(
            train_in,
            train_out,
            query_in,
            query_out,
            ids,
            in_basis,
            out_basis,
            level_table,
            in_level[None, :],
            out_level[None, :],
            lengths,
        )

    placed = (
        P("ex", "row"),
        P("ex", "col"),
        P("ex", "row"),
        P("ex", "col"),
        P("ex"),
        P("row", None, None),
        P("col", None, None),
        P(),
        P("row"),
        P("col"),
        P(),
    )
    return jax.shard_map(
        body, mesh=mesh, in_specs=placed, out_specs=(P(None, "ex"), P()), check_vma=False
    )
```

```python
import functools

import jax
import jax.numpy as jnp
from jax import lax
from jax.experimental import pallas as pl
from jax.experimental.pallas import tpu as pltpu
from jax.sharding import PartitionSpec as P

QUERIES = 2
DAMPING = 0.1
MESH = pl.DeviceIdType.MESH
F32 = jnp.float32
BF16 = jnp.bfloat16


def dot(a, b):
    return jnp.dot(a, b, preferred_element_type=F32)


def kernel(
    sizes,
    train_in,
    train_out,
    query_in,
    query_out,
    ids,
    in_basis,
    out_basis,
    table_ref,
    in_level,
    out_level,
    lengths,
    token_out,
    example_out,
    acts,
    grads,
    basis_in,
    basis_out,
    q_in,
    q_out,
    q_ids,
    hot_t,
    inverse,
    left,
    right,
    damp0,
    damp1,
    lanes,
    parts,
    sums,
    load_sem,
    q_load_sem,
    q_send_sem,
    q_fwd_sem,
    q_recv_sem,
    part_send,
    part_recv,
    sum_send,
    sum_recv,
):
    rows, cols, exs, tile = sizes
    row, col, ex = lax.axis_index("row"), lax.axis_index("col"), lax.axis_index("ex")
    in_sub, width, _ = in_basis.shape
    out_sub = out_basis.shape[0]
    tokens = train_in.shape[0]
    held = query_in.shape[0]
    group = rows * cols
    place = row * cols + col
    chips = exs // 2
    sibling = ex + 1 - 2 * lax.rem(ex, 2)

    def ex_peer(k):
        return lax.rem(ex + k, exs)

    def group_peer(k):
        other = lax.rem(place + k, group)
        return {"row": other // cols, "col": lax.rem(other, cols)}

    def slot(ref, e):
        return ref.at[pl.ds(pl.multiple_of(e * held, held), held), :]

    own = [
        pltpu.make_async_copy(src, slot(ref, ex), q_load_sem.at[n])
        for n, (src, ref) in enumerate(((query_in, q_in), (query_out, q_out)))
    ]
    for copy in own:
        copy.start()
    in_loads, out_loads = [], []
    for j in range(in_sub):
        in_loads.append(
            (
                pltpu.make_async_copy(
                    train_in.at[:, pl.ds(j * width, width)], acts.at[j], load_sem.at[0, 0, j]
                ),
                pltpu.make_async_copy(in_basis.at[j], basis_in.at[j], load_sem.at[0, 1, j]),
            )
        )
    for i in range(out_sub):
        out_loads.append(
            (
                pltpu.make_async_copy(
                    train_out.at[:, pl.ds(i * width, width)], grads.at[:, pl.ds(i * width, width)], load_sem.at[1, 0, i]
                ),
                pltpu.make_async_copy(out_basis.at[i], basis_out.at[i], load_sem.at[1, 1, i]),
            )
        )
    for pair in in_loads + out_loads:
        for copy in pair:
            copy.start()

    at_row = lax.broadcasted_iota(jnp.int32, (held, 128), 0)
    code = jnp.zeros((held, 128), jnp.int32)
    for t in range(held):
        code = jnp.where(at_row == t, ids[t], code)
    q_ids[pl.ds(pl.multiple_of(ex * held, held), held), :] = code

    barrier = pltpu.get_barrier_semaphore()
    for k in range(1, exs):
        pl.semaphore_signal(barrier, inc=1, device_id={"ex": ex_peer(k)}, device_id_type=MESH)
    for k in range(1, group):
        pl.semaphore_signal(barrier, inc=1, device_id=group_peer(k), device_id_type=MESH)
    pl.semaphore_wait(barrier, exs - 1 + group - 1)

    gathered = (q_in, q_out, q_ids)

    def move(n, e, to, send):
        return pltpu.make_async_remote_copy(
            src_ref=slot(gathered[n], e),
            dst_ref=slot(gathered[n], e),
            send_sem=send,
            recv_sem=q_recv_sem.at[n, e],
            device_id={"ex": to},
            device_id_type=MESH,
        )

    firsts = []
    for n in range(3):
        if n < len(own):
            own[n].wait()
        for k in range(1, chips):
            firsts.append(move(n, ex, ex_peer(2 * k), q_send_sem.at[n, k]))
        firsts.append(move(n, ex, sibling, q_send_sem.at[n, 0]))
        for copy in firsts[-chips:]:
            copy.start()

    for j in range(in_sub):
        for copy in in_loads[j]:
            copy.wait()
        acts[j] = dot(acts[j], basis_in[j]).astype(BF16)
    for i in range(out_sub):
        for copy in out_loads[i]:
            copy.wait()
        at = pl.ds(i * width, width)
        grads[:, at] = dot(grads[:, at], basis_out[i]).astype(BF16)

    table = 1.0 / (table_ref[...] + DAMPING)
    levels = table.shape[0]
    high = table.astype(BF16)
    low = (table - high.astype(F32)).astype(BF16)
    split = jnp.concatenate([high.astype(F32), low.astype(F32)], axis=0).astype(BF16)
    n_in, n_out = in_sub * width, out_sub * width
    in_hot = (
        lax.broadcasted_iota(jnp.int32, (levels, n_in), 0) == in_level[...]
    ).astype(F32).astype(BF16)
    spread = dot(split, in_hot).astype(BF16)
    for i in range(out_sub):
        out_hot = (
            lax.rem(lax.broadcasted_iota(jnp.int32, (2 * levels, width), 0), levels)
            == out_level[:, pl.ds(i * width, width)]
        ).astype(F32)
        hot_t[pl.ds(i * width, width), :] = out_hot.T.astype(BF16)
    step = width // 4

    def expand(k, carry):
        at = pl.ds(pl.multiple_of(k * step, step), step)
        inverse[at, :] = dot(hot_t[at, :], spread).astype(BF16)
        return carry

    whole = n_out // step
    first = whole * 5 // 8
    lax.fori_loop(0, first, expand, 0)

    forwards = []
    for n in range(3):
        for k in range(1, chips):
            source = lax.rem(ex + exs - 2 * k, exs)
            move(n, source, sibling, q_fwd_sem.at[n, k]).wait_recv()
            forwards.append(move(n, source, sibling, q_fwd_sem.at[n, k]))
            forwards[-1].start()

    lax.fori_loop(first, whole, expand, 0)

    for n in range(3):
        move(n, sibling, sibling, q_send_sem.at[n, 0]).wait_recv()
        for k in range(1, chips):
            source = lax.rem(sibling + exs - 2 * k, exs)
            move(n, source, sibling, q_send_sem.at[n, 0]).wait_recv()

    count = exs * held
    who = q_ids[:, 0:1]
    for j in range(in_sub):
        turned = dot(q_in[:, pl.ds(j * width, width)], basis_in[j])
        for q in range(QUERIES):
            right[q, :, pl.ds(j * width, width)] = jnp.where(who == q, turned, 0.0).astype(BF16)
    for i in range(out_sub):
        turned = dot(q_out[:, pl.ds(i * width, width)], basis_out[i])
        left[pl.ds(i * width, width), :] = turned.T.astype(BF16)

    damps = (damp0, damp1)
    lanes[...] = jnp.zeros_like(lanes)
    tiles = n_in // tile
    per = width // tile

    def build(q, c):
        at_c = pl.ds(pl.multiple_of(c * tile, tile), tile)
        for i in range(out_sub):
            at_r = pl.ds(i * width, width)
            rotated = dot(left[at_r, :], right[q, :, at_c])
            damps[q][at_r, :] = (rotated * inverse[at_r, at_c].astype(F32)).astype(BF16)

    def score(q, c):
        x = acts[c // per, :, pl.ds(pl.multiple_of(lax.rem(c, per) * tile, tile), tile)]
        product = dot(grads[...], damps[q][...]) * x.astype(F32)
        total = product[:, 0:128]
        for g in range(1, tile // 128):
            total = total + product[:, g * 128 : (g + 1) * 128]
        lanes[q] += total

    def outer(c, carry):
        build(1, c)
        score(0, c)
        build(0, jnp.minimum(c + 1, tiles - 1))
        score(1, c)
        return carry

    build(0, 0)
    lax.fori_loop(0, tiles, outer, 0)

    mine = jnp.concatenate(
        [jnp.sum(lanes[q].T, axis=0, keepdims=True) for q in range(QUERIES)], axis=0
    )
    parts[place] = mine
    sends = []
    for k in range(1, group):
        sends.append(
            pltpu.make_async_remote_copy(
                src_ref=parts.at[place],
                dst_ref=parts.at[place],
                send_sem=part_send.at[k],
                recv_sem=part_recv.at[place],
                device_id=group_peer(k),
                device_id_type=MESH,
            )
        )
        sends[-1].start()
    for k in range(1, group):
        source = lax.rem(place + k, group)
        pltpu.make_async_remote_copy(
            src_ref=parts.at[source],
            dst_ref=parts.at[source],
            send_sem=part_send.at[k],
            recv_sem=part_recv.at[source],
            device_id=group_peer(k),
            device_id_type=MESH,
        ).wait_recv()
    scores = jnp.sum(parts[...], axis=0)
    token_out[...] = scores

    position = ex * tokens + lax.broadcasted_iota(jnp.int32, (QUERIES, tokens), 1)
    lane = lax.broadcasted_iota(jnp.int32, (QUERIES, 128), 1)
    found = jnp.zeros((QUERIES, 128), F32)
    start = jnp.int32(0)
    for e in range(lengths.shape[0]):
        end = start + lengths[e]
        inside = (position >= start) & (position < end)
        value = jnp.sum(jnp.where(inside, scores, 0.0), axis=1, keepdims=True)
        found = jnp.where(lane == e, value, found)
        start = end
    sums[ex] = found
    for k in range(1, exs):
        sends.append(
            pltpu.make_async_remote_copy(
                src_ref=sums.at[ex],
                dst_ref=sums.at[ex],
                send_sem=sum_send.at[k],
                recv_sem=sum_recv.at[ex],
                device_id={"ex": ex_peer(k)},
                device_id_type=MESH,
            )
        )
        sends[-1].start()
    for k in range(1, exs):
        source = ex_peer(k)
        pltpu.make_async_remote_copy(
            src_ref=sums.at[source],
            dst_ref=sums.at[source],
            send_sem=sum_send.at[k],
            recv_sem=sum_recv.at[source],
            device_id={"ex": source},
            device_id_type=MESH,
        ).wait_recv()
    example_out[...] = jnp.sum(sums[...], axis=0)[:, 0 : lengths.shape[0]]
    for copy in firsts + forwards + sends:
        copy.wait_send()


def solution(mesh):
    rows, cols, exs = mesh.shape["row"], mesh.shape["col"], mesh.shape["ex"]

    def body(
        train_in,
        train_out,
        query_in,
        query_out,
        query_ids,
        in_basis,
        out_basis,
        level_table,
        in_level,
        out_level,
        lengths,
    ):
        in_sub, width, _ = in_basis.shape
        out_sub = out_basis.shape[0]
        tokens, held = train_in.shape[0], query_in.shape[0]
        count = exs * held
        n_in, n_out = in_sub * width, out_sub * width
        levels = level_table.shape[0]
        tile = width // 4
        group = rows * cols
        hbm = pl.BlockSpec(memory_space=pl.ANY)
        vmem = pl.BlockSpec(memory_space=pltpu.VMEM)
        smem = pl.BlockSpec(memory_space=pltpu.SMEM)
        most = max(in_sub, out_sub)
        dma = pltpu.SemaphoreType.DMA
        return pl.pallas_call(
            functools.partial(kernel, (rows, cols, exs, tile)),
            out_shape=(
                jax.ShapeDtypeStruct((QUERIES, tokens), F32),
                jax.ShapeDtypeStruct((QUERIES, lengths.shape[0]), F32),
            ),
            in_specs=[hbm] * 4 + [smem] + [hbm] * 2 + [vmem] * 3 + [smem],
            out_specs=(vmem, vmem),
            scratch_shapes=[
                pltpu.VMEM((in_sub, tokens, width), BF16),
                pltpu.VMEM((tokens, n_out), BF16),
                pltpu.VMEM((in_sub, width, width), BF16),
                pltpu.VMEM((out_sub, width, width), BF16),
                pltpu.VMEM((count, n_in), BF16),
                pltpu.VMEM((count, n_out), BF16),
                pltpu.VMEM((count, 128), jnp.int32),
                pltpu.VMEM((n_out, 2 * levels), BF16),
                pltpu.VMEM((n_out, n_in), BF16),
                pltpu.VMEM((n_out, count), BF16),
                pltpu.VMEM((QUERIES, count, n_in), BF16),
                pltpu.VMEM((n_out, tile), BF16),
                pltpu.VMEM((n_out, tile), BF16),
                pltpu.VMEM((QUERIES, tokens, 128), F32),
                pltpu.VMEM((group, QUERIES, tokens), F32),
                pltpu.VMEM((exs, QUERIES, 128), F32),
                dma((2, 2, most)),
                dma((3,)),
                dma((3, exs // 2)),
                dma((3, exs // 2)),
                dma((3, exs)),
                dma((group,)),
                dma((group,)),
                dma((exs,)),
                dma((exs,)),
            ],
            compiler_params=pltpu.CompilerParams(
                collective_id=0, has_side_effects=True, vmem_limit_bytes=66 * 1000 * 1000
            ),
        )(
            train_in,
            train_out,
            query_in,
            query_out,
            query_ids,
            in_basis,
            out_basis,
            level_table,
            in_level[None, :],
            out_level[None, :],
            lengths,
        )

    placed = (
        P("ex", "row"),
        P("ex", "col"),
        P("ex", "row"),
        P("ex", "col"),
        P("ex"),
        P("row", None, None),
        P("col", None, None),
        P(),
        P("row"),
        P("col"),
        P(),
    )
    return jax.shard_map(
        body, mesh=mesh, in_specs=placed, out_specs=(P(None, "ex"), P()), check_vma=False
    )
```

```python
import functools

import jax
import jax.numpy as jnp
from jax import lax
from jax.experimental import pallas as pl
from jax.experimental.pallas import tpu as pltpu
from jax.sharding import PartitionSpec as P

QUERIES = 2
DAMPING = 0.1
MESH = pl.DeviceIdType.MESH
F32 = jnp.float32
BF16 = jnp.bfloat16


def dot(a, b):
    return jnp.dot(a, b, preferred_element_type=F32)


def kernel(
    sizes,
    train_in,
    train_out,
    query_in,
    query_out,
    ids,
    in_basis,
    out_basis,
    table_ref,
    in_level,
    out_level,
    lengths,
    token_out,
    example_out,
    acts,
    grads,
    basis_in,
    basis_out,
    q_in,
    q_out,
    q_ids,
    hot_t,
    inverse,
    left,
    right,
    damp0,
    damp1,
    lanes,
    parts,
    sums,
    load_sem,
    q_load_sem,
    q_send_sem,
    q_fwd_sem,
    q_recv_sem,
    part_send,
    part_recv,
    sum_send,
    sum_recv,
):
    rows, cols, exs, tile = sizes
    row, col, ex = lax.axis_index("row"), lax.axis_index("col"), lax.axis_index("ex")
    in_sub, width, _ = in_basis.shape
    out_sub = out_basis.shape[0]
    tokens = train_in.shape[0]
    held = query_in.shape[0]
    group = rows * cols
    place = row * cols + col
    chips = exs // 2
    sibling = ex + 1 - 2 * lax.rem(ex, 2)

    def ex_peer(k):
        return lax.rem(ex + k, exs)

    def group_peer(k):
        other = lax.rem(place + k, group)
        return {"row": other // cols, "col": lax.rem(other, cols)}

    def slot(ref, e):
        return ref.at[pl.ds(pl.multiple_of(e * held, held), held), :]

    own = [
        pltpu.make_async_copy(src, slot(ref, ex), q_load_sem.at[n])
        for n, (src, ref) in enumerate(((query_in, q_in), (query_out, q_out)))
    ]
    for copy in own:
        copy.start()
    in_loads, out_loads = [], []
    for j in range(in_sub):
        in_loads.append(
            (
                pltpu.make_async_copy(
                    train_in.at[:, pl.ds(j * width, width)], acts.at[j], load_sem.at[0, 0, j]
                ),
                pltpu.make_async_copy(in_basis.at[j], basis_in.at[j], load_sem.at[0, 1, j]),
            )
        )
    for i in range(out_sub):
        out_loads.append(
            (
                pltpu.make_async_copy(
                    train_out.at[:, pl.ds(i * width, width)], grads.at[:, pl.ds(i * width, width)], load_sem.at[1, 0, i]
                ),
                pltpu.make_async_copy(out_basis.at[i], basis_out.at[i], load_sem.at[1, 1, i]),
            )
        )
    for pair in in_loads + out_loads:
        for copy in pair:
            copy.start()

    at_row = lax.broadcasted_iota(jnp.int32, (held, 128), 0)
    code = jnp.zeros((held, 128), jnp.int32)
    for t in range(held):
        code = jnp.where(at_row == t, ids[t], code)
    q_ids[pl.ds(pl.multiple_of(ex * held, held), held), :] = code

    barrier = pltpu.get_barrier_semaphore()
    for k in range(1, exs):
        pl.semaphore_signal(barrier, inc=1, device_id={"ex": ex_peer(k)}, device_id_type=MESH)
    for k in range(1, group):
        pl.semaphore_signal(barrier, inc=1, device_id=group_peer(k), device_id_type=MESH)
    pl.semaphore_wait(barrier, exs - 1 + group - 1)

    gathered = (q_in, q_out, q_ids)

    def move(n, e, to, send):
        return pltpu.make_async_remote_copy(
            src_ref=slot(gathered[n], e),
            dst_ref=slot(gathered[n], e),
            send_sem=send,
            recv_sem=q_recv_sem.at[n, e],
            device_id={"ex": to},
            device_id_type=MESH,
        )

    firsts = []
    for n in range(3):
        if n < len(own):
            own[n].wait()
        for k in range(1, chips):
            firsts.append(move(n, ex, ex_peer(2 * k), q_send_sem.at[n, k]))
        firsts.append(move(n, ex, sibling, q_send_sem.at[n, 0]))
        for copy in firsts[-chips:]:
            copy.start()

    for j in range(in_sub):
        for copy in in_loads[j]:
            copy.wait()
        acts[j] = dot(acts[j], basis_in[j]).astype(BF16)
    for i in range(out_sub):
        for copy in out_loads[i]:
            copy.wait()
        at = pl.ds(i * width, width)
        grads[:, at] = dot(grads[:, at], basis_out[i]).astype(BF16)

    table = 1.0 / (table_ref[...] + DAMPING)
    levels = table.shape[0]
    high = table.astype(BF16)
    low = (table - high.astype(F32)).astype(BF16)
    split = jnp.concatenate([high.astype(F32), low.astype(F32)], axis=0).astype(BF16)
    n_in, n_out = in_sub * width, out_sub * width
    in_hot = (
        lax.broadcasted_iota(jnp.int32, (levels, n_in), 0) == in_level[...]
    ).astype(F32).astype(BF16)
    spread = dot(split, in_hot).astype(BF16)
    for i in range(out_sub):
        out_hot = (
            lax.rem(lax.broadcasted_iota(jnp.int32, (2 * levels, width), 0), levels)
            == out_level[:, pl.ds(i * width, width)]
        ).astype(F32)
        hot_t[pl.ds(i * width, width), :] = out_hot.T.astype(BF16)
    step = width // 4

    def expand(k, carry):
        at = pl.ds(pl.multiple_of(k * step, step), step)
        inverse[at, :] = dot(hot_t[at, :], spread).astype(BF16)
        return carry

    whole = n_out // step
    first = whole * 5 // 8
    lax.fori_loop(0, first, expand, 0)

    forwards = []
    for n in range(3):
        for k in range(1, chips):
            source = lax.rem(ex + exs - 2 * k, exs)
            move(n, source, sibling, q_fwd_sem.at[n, k]).wait_recv()
            forwards.append(move(n, source, sibling, q_fwd_sem.at[n, k]))
            forwards[-1].start()

    lax.fori_loop(first, whole, expand, 0)

    for n in range(3):
        move(n, sibling, sibling, q_send_sem.at[n, 0]).wait_recv()
        for k in range(1, chips):
            source = lax.rem(sibling + exs - 2 * k, exs)
            move(n, source, sibling, q_send_sem.at[n, 0]).wait_recv()

    count = exs * held
    who = q_ids[:, 0:1]
    for j in range(in_sub):
        turned = dot(q_in[:, pl.ds(j * width, width)], basis_in[j])
        for q in range(QUERIES):
            right[q, :, pl.ds(j * width, width)] = jnp.where(who == q, turned, 0.0).astype(BF16)
    for i in range(out_sub):
        turned = dot(q_out[:, pl.ds(i * width, width)], basis_out[i])
        left[pl.ds(i * width, width), :] = turned.T.astype(BF16)

    damps = (damp0, damp1)
    lanes[...] = jnp.zeros_like(lanes)
    tiles = n_in // tile
    per = width // tile

    def build(q, c):
        at_c = pl.ds(pl.multiple_of(c * tile, tile), tile)
        for i in range(out_sub):
            at_r = pl.ds(i * width, width)
            rotated = dot(left[at_r, :], right[q, :, at_c])
            damps[q][at_r, :] = (rotated * inverse[at_r, at_c].astype(F32)).astype(BF16)

    def score(q, c):
        x = acts[c // per, :, pl.ds(pl.multiple_of(lax.rem(c, per) * tile, tile), tile)]
        product = dot(grads[...], damps[q][...]) * x.astype(F32)
        total = product[:, 0:128]
        for g in range(1, tile // 128):
            total = total + product[:, g * 128 : (g + 1) * 128]
        lanes[q] += total

    def outer(c, carry):
        build(1, c)
        score(0, c)
        build(0, jnp.minimum(c + 1, tiles - 1))
        score(1, c)
        return carry

    build(0, 0)
    lax.fori_loop(0, tiles, outer, 0)

    mine = jnp.concatenate(
        [jnp.sum(lanes[q].T, axis=0, keepdims=True) for q in range(QUERIES)], axis=0
    )
    parts[place] = mine
    sends = []
    for k in range(1, group):
        sends.append(
            pltpu.make_async_remote_copy(
                src_ref=parts.at[place],
                dst_ref=parts.at[place],
                send_sem=part_send.at[k],
                recv_sem=part_recv.at[place],
                device_id=group_peer(k),
                device_id_type=MESH,
            )
        )
        sends[-1].start()
    for k in range(1, group):
        source = lax.rem(place + k, group)
        pltpu.make_async_remote_copy(
            src_ref=parts.at[source],
            dst_ref=parts.at[source],
            send_sem=part_send.at[k],
            recv_sem=part_recv.at[source],
            device_id=group_peer(k),
            device_id_type=MESH,
        ).wait_recv()
    scores = jnp.sum(parts[...], axis=0)
    token_out[...] = scores

    position = ex * tokens + lax.broadcasted_iota(jnp.int32, (QUERIES, tokens), 1)
    lane = lax.broadcasted_iota(jnp.int32, (QUERIES, 128), 1)
    found = jnp.zeros((QUERIES, 128), F32)
    start = jnp.int32(0)
    for e in range(lengths.shape[0]):
        end = start + lengths[e]
        inside = (position >= start) & (position < end)
        value = jnp.sum(jnp.where(inside, scores, 0.0), axis=1, keepdims=True)
        found = jnp.where(lane == e, value, found)
        start = end
    sums[ex] = found
    for k in range(1, exs):
        sends.append(
            pltpu.make_async_remote_copy(
                src_ref=sums.at[ex],
                dst_ref=sums.at[ex],
                send_sem=sum_send.at[k],
                recv_sem=sum_recv.at[ex],
                device_id={"ex": ex_peer(k)},
                device_id_type=MESH,
            )
        )
        sends[-1].start()
    for k in range(1, exs):
        source = ex_peer(k)
        pltpu.make_async_remote_copy(
            src_ref=sums.at[source],
            dst_ref=sums.at[source],
            send_sem=sum_send.at[k],
            recv_sem=sum_recv.at[source],
            device_id={"ex": source},
            device_id_type=MESH,
        ).wait_recv()
    example_out[...] = jnp.sum(sums[...], axis=0)[:, 0 : lengths.shape[0]]
    for copy in firsts + forwards + sends:
        copy.wait_send()


def solution(mesh):
    rows, cols, exs = mesh.shape["row"], mesh.shape["col"], mesh.shape["ex"]

    def body(
        train_in,
        train_out,
        query_in,
        query_out,
        query_ids,
        in_basis,
        out_basis,
        level_table,
        in_level,
        out_level,
        lengths,
    ):
        in_sub, width, _ = in_basis.shape
        out_sub = out_basis.shape[0]
        tokens, held = train_in.shape[0], query_in.shape[0]
        count = exs * held
        n_in, n_out = in_sub * width, out_sub * width
        levels = level_table.shape[0]
        tile = width // 2 if 4 * count <= width else width // 4
        group = rows * cols
        hbm = pl.BlockSpec(memory_space=pl.ANY)
        vmem = pl.BlockSpec(memory_space=pltpu.VMEM)
        smem = pl.BlockSpec(memory_space=pltpu.SMEM)
        most = max(in_sub, out_sub)
        dma = pltpu.SemaphoreType.DMA
        return pl.pallas_call(
            functools.partial(kernel, (rows, cols, exs, tile)),
            out_shape=(
                jax.ShapeDtypeStruct((QUERIES, tokens), F32),
                jax.ShapeDtypeStruct((QUERIES, lengths.shape[0]), F32),
            ),
            in_specs=[hbm] * 4 + [smem] + [hbm] * 2 + [vmem] * 3 + [smem],
            out_specs=(vmem, vmem),
            scratch_shapes=[
                pltpu.VMEM((in_sub, tokens, width), BF16),
                pltpu.VMEM((tokens, n_out), BF16),
                pltpu.VMEM((in_sub, width, width), BF16),
                pltpu.VMEM((out_sub, width, width), BF16),
                pltpu.VMEM((count, n_in), BF16),
                pltpu.VMEM((count, n_out), BF16),
                pltpu.VMEM((count, 128), jnp.int32),
                pltpu.VMEM((n_out, 2 * levels), BF16),
                pltpu.VMEM((n_out, n_in), BF16),
                pltpu.VMEM((n_out, count), BF16),
                pltpu.VMEM((QUERIES, count, n_in), BF16),
                pltpu.VMEM((n_out, tile), BF16),
                pltpu.VMEM((n_out, tile), BF16),
                pltpu.VMEM((QUERIES, tokens, 128), F32),
                pltpu.VMEM((group, QUERIES, tokens), F32),
                pltpu.VMEM((exs, QUERIES, 128), F32),
                dma((2, 2, most)),
                dma((3,)),
                dma((3, exs // 2)),
                dma((3, exs // 2)),
                dma((3, exs)),
                dma((group,)),
                dma((group,)),
                dma((exs,)),
                dma((exs,)),
            ],
            compiler_params=pltpu.CompilerParams(
                collective_id=0, has_side_effects=True, vmem_limit_bytes=66 * 1000 * 1000
            ),
        )(
            train_in,
            train_out,
            query_in,
            query_out,
            query_ids,
            in_basis,
            out_basis,
            level_table,
            in_level[None, :],
            out_level[None, :],
            lengths,
        )

    placed = (
        P("ex", "row"),
        P("ex", "col"),
        P("ex", "row"),
        P("ex", "col"),
        P("ex"),
        P("row", None, None),
        P("col", None, None),
        P(),
        P("row"),
        P("col"),
        P(),
    )
    return jax.shard_map(
        body, mesh=mesh, in_specs=placed, out_specs=(P(None, "ex"), P()), check_vma=False
    )
```
